32 devices in a mesh: slab: 8 (over z, y), plane: 4 (over x, core).
Axes of the slice: x: 2, y: 2, z: 4, core: 2. Of those that a mesh axis runs over, the one named last changes fastest.
Arguments:
- tissue_v: float32 [32, 64, 128], P('slab', 'plane'), may hold values from -4 to 4
- tissue_gates: float32 [40, 32, 64, 128], P(None, 'slab', 'plane'), may hold values from 0 to 1
- tissue_diff: float32 [32, 64, 128], P('slab', 'plane'), may hold values from 0.2 to 1
- fibre_v: float32 [128, 2048], P('slab', 'plane'), may hold values from -4 to 4
- fibre_gates: float32 [40, 128, 2048], P(None, 'slab', 'plane'), may hold values from 0 to 1
- fibre_diff: float32 [128, 2048], P('slab', 'plane'), may hold values from 0.2 to 1
- gate_half: float32 [40], replicated, may hold values from -3 to 3
- gate_rate: float32 [40], replicated, may hold values from 0.5 to 20
- gate_cond: float32 [40], replicated, may hold values from 0.01 to 0.15
- gate_rev: float32 [40], replicated, may hold values from -2 to 2
- junc_cond: float32 [8], replicated, may hold values from 0.25 to 2
- junc_fibre: int32 [131072], P(('slab', 'plane')), may hold values from 0 to 15
- junc_fcell: int32 [131072], P(('slab', 'plane')), may hold values from 0 to 511
- junc_owner: int32 [131072, 1], P(('slab', 'plane')), may hold values from 0 to 31; in each aligned block of 4096 rows (0 to 4095, 4096 to 8191, ...) at most 256 rows name the same one
- junc_tcell: int32 [131072], P(('slab', 'plane')), may hold values from 0 to 8191
- junc_class: int32 [131072], P(('slab', 'plane')), may hold values from 0 to 7
Outputs:
- tissue_out: float32 [32, 64, 128], P('slab', 'plane')
- fibre_out: float32 [128, 2048], P('slab', 'plane')
The draws below stay inside these ranges and needn't reach their ends.
Inputs may be any that keep to these rules, and one draw needn't show every extreme that they name: `junc_owner`: among the junctions held by one device, no tissue block is named by more than 256 of them, and some block is named by exactly 256. `junc_fibre`: A fibre of the slab group of the device that holds the junction. `junc_fcell`: A cell of the holding device's share of that fibre. `junc_tcell`: numbered over the owner's block in the order z, y, x with x fastest.
All inputs are finite; a program needn't handle non-finite values.
Results may differ from the reference program's by a relative error of at most 0.00005.
Values sent between devices are 32-bit elements; how exact they have to be, the bound alone decides.
A program may use at most 64 MiB of HBM per device.

```python
import math
import jax
import jax.numpy as jnp
import numpy as np
from jax import lax

NX = 128
CY = 16
CZ = 4
FIB_DEV = 16
FCELLS = 2048
GATES = 40
CLASSES = 8
STEPS = 14
JUNC_DEV = 4096
CAP = 256
NZ = 32
NY = 64
NFIB = 128
JUNCS = 131072
N_PLANE = 4
DEVICES = 32


def set_ends(result, own_key, least, high):
    dims = result.shape
    index_at = [jax.random.randint(jax.random.fold_in(own_key, axis), (), 0, dims[axis]) for axis in range(len(dims))]
    result = result.at[tuple(index_at)].set(least)
    longest = dims.index(max(dims))
    index_at[longest] = (index_at[longest] + 1) % dims[longest]
    return result.at[tuple(index_at)].set(high)


def block_scale(rng, dims, pieces, smallest, largest):
    gain, own = 1.0, jax.random.fold_in(rng, 6)
    for axis_at, blocks in pieces:
        draws = jnp.exp(jax.random.uniform(jax.random.fold_in(own, axis_at), (blocks,), jnp.float32, smallest / len(pieces), largest / len(pieces)))
        gain = gain * jnp.repeat(draws, dims[axis_at] // blocks).reshape([-1 if axis == axis_at else 1 for axis in range(len(dims))])
    return gain


def shared_out(rng, own, number, rows, amount, top, reach, lean):
    ranking = jax.random.permutation(rng, amount)
    packed, usual = shares(amount, rows * top, reach, lean, True), shares(amount, rows * top, reach, lean, False)
    places = jnp.arange(amount)

    def named(sizes, rotation):
        used = int((sizes > 0).sum())
        fixed = max(1, used // 4)
        moved = fixed + (places - fixed + rotation * (used - fixed)) % max(1, amount - fixed)
        return jnp.zeros((amount,), jnp.int32).at[ranking[jnp.where(places < fixed, places, moved)]].set(jnp.asarray(sizes, jnp.int32))

    sizes = jnp.where(number % 4 == 0, named(packed, number // 4), named(usual, number - number // 4 - 1))
    mixed = jax.random.permutation(jax.random.fold_in(own, 3), amount)
    giver, sink = mixed[0:amount // 2 * 2:2], mixed[1:amount // 2 * 2:2]
    room = jnp.minimum(sizes[giver] - 1, reach - sizes[sink]) // 2
    room = jnp.where((giver == ranking[0]) | (sink == ranking[0]) | (sizes[sink] == 0), 0, jnp.maximum(room, 0))
    moved = jax.random.randint(jax.random.fold_in(own, 4), (amount // 2,), 0, 1 << 20) % (room + 1)
    sizes = sizes.at[giver].add(-moved).at[sink].add(moved)
    items = jnp.searchsorted(jnp.cumsum(sizes), jnp.arange(rows * top), side="right").astype(jnp.int32)
    table = items.reshape(top, rows).T
    table = table[jax.random.permutation(jax.random.fold_in(own, 1), rows)]
    rotation = jax.random.randint(jax.random.fold_in(own, 2), (rows, 1), 0, top)
    return jnp.take_along_axis(table, (jnp.arange(top)[None, :] + rotation) % top, axis=1)


def shares(count, total, limit, lean, full):
    loads = [(1 << 20) // math.isqrt(grade ** lean) + 1 for grade in range(1, count + 1)]
    largest = limit if full else min(limit, max(-(-total // count), total * loads[0] // sum(loads)))
    least = 1 if total - largest >= count - 1 else 0
    holding, surplus = [largest] + [least] * (count - 1), total - largest - least * (count - 1)
    while surplus > 0:
        candidates = [i for i in range(1, count) if holding[i] < largest] or [i for i in range(1, count) if holding[i] < limit]
        mass, remaining = sum([loads[i] for i in candidates]), surplus
        for i in candidates:
            extra = min(limit - holding[i], max(1, remaining * loads[i] // mass), surplus)
            holding[i] = holding[i] + extra
            surplus = surplus - extra
    return np.array(holding)


def centred(rng, shape, scale, bound, split=(), kind=jnp.bfloat16):
    drawn = jax.random.normal(rng, shape, jnp.float32) * scale
    if len(split) > 0:
        drawn = block_scale(rng, shape, split, -0.22, 0.18) * drawn
    return jnp.clip(drawn, min=-bound, max=bound).astype(kind)


def setup_inputs(seed: int = 0) -> dict:
    splits = jax.random.split(jax.random.key(seed), 17)
    tissue_v = centred(splits[0], (NZ, NY, NX), 1.0, 4.0, ((0, 8), (1, 4)), jnp.float32)
    tissue_gates = jnp.clip(1.0 * jax.random.uniform(splits[1], (GATES, NZ, NY, NX), jnp.float32) ** block_scale(splits[1], (GATES, NZ, NY, NX), ((1, 8), (2, 4)), -0.2, 0.2), 0.0, 1.0)
    tissue_diff = jnp.clip(jnp.exp(math.log(1.0) - 1.609438 * jax.random.uniform(splits[2], (NZ, NY, NX), jnp.float32) ** block_scale(splits[2], (NZ, NY, NX), ((0, 8), (1, 4)), -0.2, 0.2)), 0.2, 1.0)
    fibre_v = centred(splits[3], (NFIB, FCELLS), 1.0, 4.0, ((0, 8), (1, 4)), jnp.float32)
    fibre_gates = jnp.clip(1.0 * jax.random.uniform(splits[4], (GATES, NFIB, FCELLS), jnp.float32) ** block_scale(splits[4], (GATES, NFIB, FCELLS), ((1, 8), (2, 4)), -0.2, 0.2), 0.0, 1.0)
    fibre_diff = jnp.clip(jnp.exp(math.log(1.0) - 1.609438 * jax.random.uniform(splits[5], (NFIB, FCELLS), jnp.float32) ** block_scale(splits[5], (NFIB, FCELLS), ((0, 8), (1, 4)), -0.2, 0.2)), 0.2, 1.0)
    gate_half = centred(splits[6], (GATES,), 1.0, 3.0, (), jnp.float32)
    gate_rate = jnp.clip(jnp.exp(jax.random.uniform(splits[7], (GATES,), jnp.float32, math.log(0.5), math.log(20.0))), 0.5, 20.0)
    gate_cond = jnp.clip(jnp.exp(jax.random.uniform(splits[8], (GATES,), jnp.float32, math.log(0.01), math.log(0.15))), 0.01, 0.15)
    gate_rev = jnp.clip(jax.random.uniform(splits[9], (GATES,), jnp.float32, -2.0, 2.0), -2.0, 2.0)
    junc_cond = jnp.clip(jnp.exp(jax.random.uniform(splits[10], (CLASSES,), jnp.float32, math.log(0.25), math.log(2.0))), 0.25, 2.0)
    junc_fibre = set_ends(jax.random.randint(splits[11], (JUNCS,), 0, FIB_DEV), jax.random.fold_in(splits[11], 1), 0, FIB_DEV - 1).astype(jnp.int32)
    junc_fcell = set_ends(jax.random.randint(splits[12], (JUNCS,), 0, FCELLS // N_PLANE), jax.random.fold_in(splits[12], 1), 0, (FCELLS // N_PLANE) - 1).astype(jnp.int32)
    junc_owner_keys = jax.random.split(jax.random.fold_in(splits[13], 1), JUNCS // JUNC_DEV)
    junc_owner_turns = jax.random.permutation(jax.random.fold_in(splits[13], 3), JUNCS // JUNC_DEV)
    junc_owner = jax.vmap(lambda own, number: shared_out(jax.random.fold_in(splits[13], 2), own, number, JUNC_DEV, DEVICES, 1, CAP, 2))(junc_owner_keys, junc_owner_turns).reshape((JUNCS, 1))
    junc_tcell = set_ends(jax.random.randint(splits[14], (JUNCS,), 0, CZ * CY * NX), jax.random.fold_in(splits[14], 1), 0, (CZ * CY * NX) - 1).astype(jnp.int32)
    junc_class = set_ends(jax.random.randint(splits[15], (JUNCS,), 0, CLASSES), jax.random.fold_in(splits[15], 1), 0, CLASSES - 1).astype(jnp.int32)
    return {"tissue_v": tissue_v, "tissue_gates": tissue_gates, "tissue_diff": tissue_diff, "fibre_v": fibre_v, "fibre_gates": fibre_gates, "fibre_diff": fibre_diff, "gate_half": gate_half, "gate_rate": gate_rate, "gate_cond": gate_cond, "gate_rev": gate_rev, "junc_cond": junc_cond, "junc_fibre": junc_fibre, "junc_fcell": junc_fcell, "junc_owner": junc_owner, "junc_tcell": junc_tcell, "junc_class": junc_class}


time_step = 0.1
gate_slope = 2.0


def membrane(voltage, gates, gate_half, gate_rate, gate_cond, gate_rev):
    gate_signs = jnp.where(jnp.arange(GATES, dtype=jnp.int32) % 2 == 0, 1.0, -1.0).astype(jnp.float32)

    def one_gate(totals, inputs):
        gate_now, mid_point, speed, conductance, reversal, direction = inputs
        shifted = voltage - mid_point
        steady = jax.nn.sigmoid(direction * gate_slope * shifted)
        decay_factor = jnp.exp(-time_step * speed * (1.0 + jax.nn.sigmoid(shifted)))
        renewed = steady + (gate_now - steady) * decay_factor
        return (totals[0] + conductance * renewed, totals[1] + (conductance * reversal) * renewed), renewed

    zero_field = jnp.zeros_like(voltage)
    sums, renewed_all = lax.scan(one_gate, (zero_field, zero_field), (gates, gate_half, gate_rate, gate_cond, gate_rev, gate_signs))
    ionic = voltage * sums[0] - sums[1]
    return renewed_all, ionic


def line_count(length):
    places = jnp.arange(length, dtype=jnp.int32)
    return (places > 0).astype(jnp.float32) + (places < length - 1).astype(jnp.float32)


def reference(tissue_v, tissue_gates, tissue_diff, fibre_v, fibre_gates, fibre_diff, gate_half, gate_rate, gate_cond, gate_rev, junc_cond, junc_fibre, junc_fcell, junc_owner, junc_tcell, junc_class):
    depth_all, height_all, width_all = tissue_v.shape
    fibre_total, fibre_len = fibre_v.shape
    share = fibre_len // N_PLANE
    total_junctions = junc_fibre.shape[0]
    holder = jnp.arange(total_junctions, dtype=jnp.int32) // JUNC_DEV
    fibre_row = (holder // N_PLANE) * FIB_DEV + junc_fibre
    fibre_col = (holder % N_PLANE) * share + junc_fcell
    fibre_flat = (fibre_row * fibre_len + fibre_col).astype(jnp.int32)
    owners = junc_owner[:, 0]
    layer_z = (owners // N_PLANE) * CZ + junc_tcell // (CY * NX)
    row_y = (owners % N_PLANE) * CY + (junc_tcell // NX) % CY
    tissue_flat = ((layer_z * height_all + row_y) * width_all + junc_tcell % NX).astype(jnp.int32)
    coupling = jnp.sum(jnp.where(junc_class[:, None] == jnp.arange(CLASSES, dtype=jnp.int32)[None, :], junc_cond[None, :], jnp.zeros((), jnp.float32)), axis=1)
    tissue_count = line_count(depth_all)[:, None, None] + line_count(height_all)[None, :, None] + line_count(width_all)[None, None, :]
    fibre_count = line_count(fibre_len)[None, :]

    def advance(carry, unused):
        tissue_now, tissue_state, fibre_now, fibre_state = carry
        tissue_line = tissue_now.reshape(-1)
        fibre_line = fibre_now.reshape(-1)
        current = coupling * (fibre_line[fibre_flat] - tissue_line[tissue_flat])
        tissue_source = jnp.zeros_like(tissue_line).at[tissue_flat].add(current).reshape(tissue_now.shape)
        fibre_source = jnp.zeros_like(fibre_line).at[fibre_flat].add(-current).reshape(fibre_now.shape)
        padded = jnp.pad(tissue_now, 1)
        neighbours = padded[2:, 1:-1, 1:-1] + padded[:-2, 1:-1, 1:-1] + padded[1:-1, 2:, 1:-1] + padded[1:-1, :-2, 1:-1] + padded[1:-1, 1:-1, 2:] + padded[1:-1, 1:-1, :-2]
        tissue_lap = neighbours - tissue_count * tissue_now
        fibre_padded = jnp.pad(fibre_now, ((0, 0), (1, 1)))
        fibre_lap = fibre_padded[:, 2:] + fibre_padded[:, :-2] - fibre_count * fibre_now
        tissue_state, tissue_ionic = membrane(tissue_now, tissue_state, gate_half, gate_rate, gate_cond, gate_rev)
        fibre_state, fibre_ionic = membrane(fibre_now, fibre_state, gate_half, gate_rate, gate_cond, gate_rev)
        tissue_next = tissue_now + time_step * (tissue_diff * tissue_lap - tissue_ionic + tissue_source)
        fibre_next = fibre_now + time_step * (fibre_diff * fibre_lap - fibre_ionic + fibre_source)
        return (tissue_next, tissue_state, fibre_next, fibre_state), None

    final, unused_out = lax.scan(advance, (tissue_v, tissue_gates, fibre_v, fibre_gates), None, length=STEPS)
    return final[0], final[2]
```

```python
import jax
import jax.numpy as jnp
from jax import lax
from jax.sharding import PartitionSpec as P

STEPS = 14


time_step = 0.1
gate_slope = 2.0


def shift_pair(up, down, axis):
    count = lax.axis_size(axis)
    forward = [(i, i + 1) for i in range(count - 1)]
    backward = [(target, source) for source, target in forward]
    return lax.ppermute(up, axis, forward), lax.ppermute(down, axis, backward)


def membrane(voltage, gates, gate_half, gate_rate, gate_cond, gate_rev):
    gate_shape = (gates.shape[0],) + (1,) * (gates.ndim - 1)
    gate_signs = (
        jnp.where(jnp.arange(gates.shape[0], dtype=jnp.int32) % 2 == 0, 1.0, -1.0)
        .astype(jnp.float32)
        .reshape(gate_shape)
    )
    shifted = voltage[None] - gate_half.reshape(gate_shape)
    steady = jax.nn.sigmoid(gate_signs * gate_slope * shifted)
    decay_factor = jnp.exp(
        -time_step * gate_rate.reshape(gate_shape) * (1.0 + jax.nn.sigmoid(shifted))
    )
    renewed = steady + (gates - steady) * decay_factor
    driving = gate_cond.reshape(gate_shape) * (voltage[None] - gate_rev.reshape(gate_shape))
    return (renewed, jnp.sum(driving * renewed, axis=0))


def line_count(length, offset, total):
    places = offset + jnp.arange(length, dtype=jnp.int32)
    return (places > 0).astype(jnp.float32) + (places < total - 1).astype(jnp.float32)


def class_gain(classes, junc_cond):
    return jnp.sum(
        jnp.where(
            classes[:, None] == jnp.arange(junc_cond.shape[0], dtype=jnp.int32)[None, :],
            junc_cond[None, :],
            jnp.zeros((), jnp.float32),
        ),
        axis=1,
    )


def make_onehot(indices, count):
    return (indices[:, None] == jnp.arange(count, dtype=jnp.int32)[None, :]).astype(jnp.float32)


def split_two(values):
    high = lax.reduce_precision(values, 8, 7)
    low = lax.reduce_precision(values - high, 8, 7)
    return high, low


def pick_split(rows, cols, table):
    depth, width = table.shape
    high, low = split_two(table)
    stacked = jnp.concatenate([high, low], axis=0).astype(jnp.bfloat16)
    onehot = rows[:, None] == (jnp.arange(2 * depth, dtype=jnp.int32) % depth)[None, :]
    rows_read = jnp.dot(
        onehot.astype(jnp.bfloat16), stacked, preferred_element_type=jnp.float32
    )
    chosen = cols[:, None] == jnp.arange(width, dtype=jnp.int32)[None, :]
    return jnp.sum(jnp.where(chosen, rows_read, 0.0), axis=1)


def place_split(rows, cols, values, depth, width):
    high, low = split_two(values)
    lanes = jnp.arange(2 * width, dtype=jnp.int32)
    both = jnp.where((lanes < width)[None, :], high[:, None], low[:, None])
    weighted = jnp.where(cols[:, None] == (lanes % width)[None, :], both, 0.0)
    onehot = (rows[:, None] == jnp.arange(depth, dtype=jnp.int32)[None, :]).astype(jnp.bfloat16)
    halves = lax.dot_general(
        onehot,
        weighted.astype(jnp.bfloat16),
        (((0,), (0,)), ((), ())),
        preferred_element_type=jnp.float32,
    )
    return halves[:, :width] + halves[:, width:]


def running_rank(owner_onehot):
    total, kinds = owner_onehot.shape
    tall = 128
    blocks = owner_onehot.astype(jnp.bfloat16).reshape(total // tall, tall, kinds)
    lower = jnp.tril(jnp.ones((tall, tall), jnp.bfloat16))
    within = jnp.einsum("ij,bjo->bio", lower, blocks, preferred_element_type=jnp.float32)
    sums = within[:, -1, :]
    count = total // tall
    before = jnp.tril(jnp.ones((count, count), jnp.float32), -1)
    ahead = jnp.dot(before, sums, precision=lax.Precision.HIGHEST)
    ranks = jnp.sum((within + ahead[:, None, :]).reshape(total, kinds) * owner_onehot, axis=1)
    return jnp.round(ranks).astype(jnp.int32) - 1


def place_values(row_onehot, col_onehot, values):
    weighted = col_onehot * values[:, None]
    return lax.dot_general(
        row_onehot,
        weighted,
        (((0,), (0,)), ((), ())),
        precision=lax.Precision.HIGHEST,
        preferred_element_type=jnp.float32,
    )


def trade_both(paired):
    return lax.all_to_all(paired, ("slab", "plane"), split_axis=1, concat_axis=1, tiled=True)


def body(
    tissue_v,
    tissue_gates,
    tissue_diff,
    fibre_v,
    fibre_gates,
    fibre_diff,
    gate_half,
    gate_rate,
    gate_cond,
    gate_rev,
    junc_cond,
    junc_fibre,
    junc_fcell,
    junc_owner,
    junc_tcell,
    junc_class,
):
    slab_count = lax.axis_size("slab")
    plane_count = lax.axis_size("plane")
    devices = slab_count * plane_count
    layers_dev, rows_dev, cols_dev = tissue_v.shape
    fibre_rows, fibre_cols = fibre_v.shape
    junctions = junc_fibre.shape[0]
    capacity = 2 * junctions // devices
    tissue_count = (
        line_count(layers_dev, lax.axis_index("slab") * layers_dev, layers_dev * slab_count)[
            :, None, None
        ]
        + line_count(rows_dev, lax.axis_index("plane") * rows_dev, rows_dev * plane_count)[
            None, :, None
        ]
        + line_count(cols_dev, 0, cols_dev)[None, None, :]
    )
    fibre_count = line_count(
        fibre_cols, lax.axis_index("plane") * fibre_cols, fibre_cols * plane_count
    )[None, :]
    fibre_cells = fibre_rows * fibre_cols
    fibre_width = 128
    fibre_grid_rows = fibre_cells // fibre_width
    tissue_grid_rows = layers_dev * rows_dev
    owners = junc_owner[:, 0]
    owner_onehot = make_onehot(owners, devices)
    rank_onehot = make_onehot(running_rank(owner_onehot), capacity)
    kinds = junc_cond.shape[0] + 1
    code = (junc_tcell * kinds + junc_class + 1).astype(jnp.float32)
    code_table = jnp.round(place_values(owner_onehot, rank_onehot, code)).astype(jnp.int32)
    fibre_index = (junc_fibre * fibre_cols + junc_fcell).astype(jnp.float32)
    fibre_table = jnp.round(place_values(owner_onehot, rank_onehot, fibre_index))
    own_cells = fibre_table.astype(jnp.int32).reshape(-1)
    sent_tables = jnp.stack([code_table // kinds, code_table % kinds - 1])
    got_tables = lax.all_to_all(
        sent_tables, ("slab", "plane"), split_axis=1, concat_axis=1, tiled=True
    )
    remote_cells = got_tables[0].reshape(-1)
    remote_gain = class_gain(got_tables[1].reshape(-1), junc_cond)
    own_gain = class_gain(sent_tables[1].reshape(-1), junc_cond)
    fibre_at_row, fibre_at_col = own_cells // fibre_width, own_cells % fibre_width
    cell_row, cell_col = remote_cells // cols_dev, remote_cells % cols_dev

    def advance(step_index, carry):
        tissue_now, tissue_state, fibre_now, fibre_state = carry
        fibre_grid = fibre_now.reshape(fibre_grid_rows, fibre_width)
        tissue_grid = tissue_now.reshape(tissue_grid_rows, cols_dev)
        end_pad = (0, cols_dev - fibre_rows)
        up = jnp.concatenate([tissue_now[:, -1], jnp.pad(fibre_now[:, -1], end_pad)[None]])
        down = jnp.concatenate([tissue_now[:, 0], jnp.pad(fibre_now[:, 0], end_pad)[None]])
        y_low, y_high = shift_pair(up, down, "plane")
        z_low, z_high = shift_pair(tissue_now[-1:], tissue_now[:1], "slab")
        fibre_at_slot = pick_split(fibre_at_row, fibre_at_col, fibre_grid)
        tissue_at_slot = pick_split(cell_row, cell_col, tissue_grid)
        paired = jnp.stack([fibre_at_slot, tissue_at_slot]).reshape(2, devices, capacity)
        traded = trade_both(paired).reshape(2, -1)
        current = remote_gain * (traded[0] - tissue_at_slot)
        fibre_current = own_gain * (fibre_at_slot - traded[1])
        tissue_source = place_split(
            cell_row, cell_col, current, tissue_grid_rows, cols_dev
        ).reshape(tissue_now.shape)
        fibre_source = place_split(
            fibre_at_row, fibre_at_col, fibre_current, fibre_grid_rows, fibre_width
        ).reshape(fibre_now.shape)
        sides = jnp.pad(tissue_now, ((0, 0), (0, 0), (1, 1)))
        neighbours = (
            jnp.concatenate([tissue_now[1:], z_high], axis=0)
            + jnp.concatenate([z_low, tissue_now[:-1]], axis=0)
            + jnp.concatenate([tissue_now[:, 1:], y_high[:-1, None]], axis=1)
            + jnp.concatenate([y_low[:-1, None], tissue_now[:, :-1]], axis=1)
            + sides[:, :, 2:]
            + sides[:, :, :-2]
        )
        tissue_lap = neighbours - tissue_count * tissue_now
        fibre_lap = (
            jnp.concatenate([fibre_now[:, 1:], y_high[-1, :fibre_rows, None]], axis=1)
            + jnp.concatenate([y_low[-1, :fibre_rows, None], fibre_now[:, :-1]], axis=1)
            - fibre_count * fibre_now
        )
        tissue_state, tissue_ionic = membrane(
            tissue_now, tissue_state, gate_half, gate_rate, gate_cond, gate_rev
        )
        fibre_state, fibre_ionic = membrane(
            fibre_now, fibre_state, gate_half, gate_rate, gate_cond, gate_rev
        )
        tissue_next = tissue_now + time_step * (
            tissue_diff * tissue_lap - tissue_ionic + tissue_source
        )
        fibre_next = fibre_now + time_step * (fibre_diff * fibre_lap - fibre_ionic - fibre_source)
        return (tissue_next, tissue_state, fibre_next, fibre_state)

    final = lax.fori_loop(0, STEPS, advance, (tissue_v, tissue_gates, fibre_v, fibre_gates))
    return (final[0], final[2])


def solution(mesh):
    in_specs = (
        P("slab", "plane", None),
        P(None, "slab", "plane", None),
        P("slab", "plane", None),
        P("slab", "plane"),
        P(None, "slab", "plane"),
        P("slab", "plane"),
        P(),
        P(),
        P(),
        P(),
        P(),
        P(("slab", "plane")),
        P(("slab", "plane")),
        P(("slab", "plane"), None),
        P(("slab", "plane")),
        P(("slab", "plane")),
    )
    out_specs = (P("slab", "plane", None), P("slab", "plane"))
    return jax.shard_map(body, mesh=mesh, in_specs=in_specs, out_specs=out_specs, check_vma=False)
```
